32 devices in a mesh: group: 4 (over z), shard: 8 (over y, x, core).
Axes of the slice: x: 2, y: 2, z: 4, core: 2. Of those that a mesh axis runs over, the one named last changes fastest.
Arguments:
- query_hidden: bfloat16 [32, 32, 768], P(('group', 'shard')), may hold values from -6 to 6
- positive_hidden: bfloat16 [32, 64, 768], P(('group', 'shard')), may hold values from -6 to 6
- passage_store: bfloat16 [256, 64, 768], P('shard'), may hold values from -6 to 6
- negative_ids: int32 [32, 8], P(('group', 'shard')), may hold values from 0 to 255, as said below
- teacher_margins: int32 [32, 8], P(('group', 'shard')), may hold values from -4096 to 4095
- transform_weight: bfloat16 [768, 768], replicated, may hold values from -0.21875 to 0.21875
- vocab_weight: bfloat16 [768, 15360], P(None, 'shard'), may hold values from -0.21875 to 0.21875
- dense_weight: bfloat16 [768, 768], replicated, may hold values from -0.21875 to 0.21875
Outputs:
- student_margin: float32 [32, 8], P(('group', 'shard'))
- dense_grad: float32 [768, 768], replicated
The draws below stay inside these ranges and needn't reach their ends.
Inputs may be any that keep to these rules, and one draw needn't show every extreme that they name: `negative_ids`: passage p is held by shard index p // 32. Among the 8 negatives of one index of group and shard, every store index is named by none or exactly 2 of them; one store index, drawn from the seed, is named 2 times by every index of group and shard.
All inputs are finite; a program needn't handle non-finite values.
Results may differ from the reference program's by a relative error of at most 0.0029.
Values may be sent and summed in bfloat16 or wider, within the bound.
A program may use at most 128 MiB of HBM per device.

```python
import math
import jax
import jax.numpy as jnp
from jax import lax

D = 768
LQ = 32
LP = 64
NEG = 8
CAP = 2
TRI_DEV = 1
STORE_DEV = 32
VOCAB = 15360
QUERIES = 32
PASSAGES = 256


def draw_negative_ids(key, part):
    owners = PASSAGES // STORE_DEV
    per_device = TRI_DEV * NEG
    blocks = QUERIES // TRI_DEV
    picked_count = per_device // CAP
    keys = jax.random.split(jax.random.fold_in(key, 31), 5)
    heat = jax.random.randint(keys[0], (owners,), 0, 4)
    heat = heat * heat * 256
    hottest = jax.random.randint(keys[1], (), 0, owners)
    heat = jnp.where(jnp.arange(owners) == hottest, 1 << 20, heat)
    noise = jax.random.randint(keys[2], (blocks, owners), 0, 1024)
    block_index = jnp.arange(blocks)[:, None]
    owner_index = jnp.arange(owners)[None, :]
    first_boost = (block_index == 0) & (owner_index == owners - 1)
    last_boost = (block_index == blocks - 1) & (owner_index == 0)
    boost = jnp.where(first_boost | last_boost, 1 << 19, 0)
    scores = (noise + boost + heat[None, :]) * owners + owner_index
    picked = lax.top_k(scores, picked_count)[1]
    owner_slots = jnp.repeat(picked, CAP, axis=1, total_repeat_length=per_device)
    order_key = jax.random.randint(keys[3], (blocks, per_device), 0, 4096) * per_device + jnp.arange(per_device)[None, :]
    order = jnp.argsort(order_key, axis=1, stable=True)
    owner_slots = jnp.take_along_axis(owner_slots, order, axis=1)
    local_rows = jax.random.randint(keys[4], (blocks, per_device), 0, STORE_DEV)
    local_rows = jnp.where((block_index == 0) & (owner_slots == owners - 1), STORE_DEV - 1, local_rows)
    local_rows = jnp.where((block_index == blocks - 1) & (owner_slots == 0), 0, local_rows)
    return (owner_slots * STORE_DEV + local_rows).reshape(QUERIES, NEG).astype(jnp.int32)


def set_ends(entries, stream_key, low, top_value):
    spot = [jax.random.randint(jax.random.fold_in(stream_key, axis), (), 0, length) for axis, length in enumerate(entries.shape)]
    widest = entries.shape.index(max(entries.shape))
    neighbour = spot[:widest] + [(spot[widest] + 1) % entries.shape[widest]] + spot[widest + 1:]
    return entries.at[tuple(spot)].set(low).at[tuple(neighbour)].set(top_value)


def block_scale(own_key, shape, pieces, smallest, high):
    def one(position, shards_of):
        draws = jax.random.uniform(jax.random.fold_in(jax.random.fold_in(own_key, 6), position), (shards_of,), jnp.float32, smallest / len(pieces), high / len(pieces))
        return jnp.repeat(jnp.exp(draws), shape[position] // shards_of).reshape((-1,) + (1,) * (len(shape) - position - 1))

    loudness = one(*pieces[0])
    for cut in pieces[1:]:
        loudness = loudness * one(*cut)
    return loudness


def normal_values(key, extent, scale, bound, pieces=(), kind=jnp.bfloat16):
    gain = block_scale(key, extent, pieces, -0.22, 0.18) if pieces else 1.0
    values = jax.random.normal(key, extent, jnp.float32) * scale * gain
    return jnp.minimum(jnp.maximum(values, -bound), bound).astype(kind)


def setup_inputs(seed: int = 0) -> dict:
    key_list = jax.random.split(jax.random.key(seed), 9)
    query_hidden = normal_values(key_list[0], (QUERIES, LQ, D), 1.0, 6.0, ((0, 32),))
    positive_hidden = normal_values(key_list[1], (QUERIES, LP, D), 1.0, 6.0, ((0, 32),))
    passage_store = normal_values(key_list[2], (PASSAGES, LP, D), 1.0, 6.0, ((0, 8),))
    negative_ids = draw_negative_ids(jax.random.fold_in(key_list[8], 71), 0)
    teacher_margins = set_ends(jax.random.randint(key_list[4], (QUERIES, NEG), -4096, 4096), jax.random.fold_in(key_list[4], 1), -4096, 4095).astype(jnp.int32)
    transform_weight = normal_values(key_list[5], (D, D), D ** -0.5, 0.21875)
    vocab_weight = normal_values(key_list[6], (D, VOCAB), D ** -0.5, 0.21875, ((1, 8),))
    dense_weight = normal_values(key_list[7], (D, D), D ** -0.5, 0.21875)
    return dict(query_hidden=query_hidden, positive_hidden=positive_hidden, passage_store=passage_store, negative_ids=negative_ids, teacher_margins=teacher_margins, transform_weight=transform_weight, vocab_weight=vocab_weight, dense_weight=dense_weight)


def encode(hidden, transform_weight):
    mixed_rows = jnp.dot(hidden, transform_weight, preferred_element_type=jnp.float32)
    active = jax.nn.gelu(mixed_rows, approximate=False)
    centre = lax.optimization_barrier(jnp.mean(active, axis=-1, keepdims=True))
    spread = lax.optimization_barrier(jnp.mean(jnp.square(active - centre), axis=-1, keepdims=True))
    return ((active - centre) * lax.rsqrt(spread + 1e-05)).astype(jnp.bfloat16)

def pool_rows(coded, vocab_weight):
    logits = jnp.dot(coded, vocab_weight, preferred_element_type=jnp.float32)
    return lax.optimization_barrier(jnp.max(jnp.log1p(jnp.maximum(logits, 0.0)), axis=-2))

def reference(query_hidden, positive_hidden, passage_store, negative_ids, teacher_margins, transform_weight, vocab_weight, dense_weight):
    negative_hidden = passage_store[negative_ids]
    passages = jnp.concatenate([positive_hidden[:, None], negative_hidden], axis=1)

    def one_query(pair):
        query_seq, passage_seqs = pair
        query_pool = pool_rows(encode(query_seq, transform_weight), vocab_weight)
        passage_pool = pool_rows(encode(passage_seqs, transform_weight), vocab_weight)
        return jnp.dot(passage_pool, query_pool, precision=lax.Precision.HIGHEST)
    sparse = lax.map(one_query, (query_hidden, passages)) / math.sqrt(VOCAB)
    inv_root = 1.0 / math.sqrt(D)
    query_cls = query_hidden[:, 0, :]
    positive_cls = positive_hidden[:, 0, :]
    negative_cls = negative_hidden[:, :, 0, :]
    query_vec = jnp.dot(query_cls, dense_weight, preferred_element_type=jnp.float32)
    positive_vec = jnp.dot(positive_cls, dense_weight, preferred_element_type=jnp.float32)
    negative_vec = jnp.dot(negative_cls, dense_weight, preferred_element_type=jnp.float32)
    dense_pos = lax.optimization_barrier(jnp.sum(query_vec * positive_vec, axis=1)) * inv_root
    dense_neg = jnp.einsum('qd,qkd->qk', query_vec, negative_vec, precision=lax.Precision.HIGHEST) * inv_root
    pos_score = sparse[:, 0] + dense_pos
    neg_score = sparse[:, 1:] + dense_neg
    margin = pos_score[:, None] - neg_score
    target = teacher_margins.astype(jnp.float32) / 1024.0
    coef = (margin - target) / NEG
    coef_total = lax.optimization_barrier(jnp.sum(coef, axis=1))
    grad_query = (coef_total[:, None] * positive_vec - jnp.einsum('qk,qkd->qd', coef, negative_vec, precision=lax.Precision.HIGHEST)) * inv_root
    grad_positive = coef_total[:, None] * query_vec * inv_root
    grad_negative = -coef[:, :, None] * query_vec[:, None, :] * inv_root
    states = jnp.concatenate([query_cls, positive_cls, negative_cls.reshape(-1, D)], axis=0).astype(jnp.float32)
    factors = jnp.concatenate([grad_query, grad_positive, grad_negative.reshape(-1, D)], axis=0)
    dense_grad = jnp.einsum('rd,re->de', states, factors, precision=lax.Precision.HIGHEST)
    return (margin, dense_grad)
```

```python
import functools
import math

import jax
import jax.numpy as jnp
from jax import lax
from jax.experimental import pallas as pl
from jax.experimental.pallas import tpu as pltpu
from jax.sharding import PartitionSpec as P

LANES = 256
COLS = 512
TILE_ROWS = 512
CHUNK_PASSAGES = 2
HIGHEST = lax.Precision.HIGHEST
MESH_ID = pl.DeviceIdType.MESH


def encode(hidden, transform_weight):
    mixed = jnp.dot(hidden, transform_weight, preferred_element_type=jnp.float32)
    active = 0.5 * mixed * (1.0 + lax.erf(mixed * math.sqrt(0.5)))
    centre = jnp.mean(active, axis=-1, keepdims=True)
    shifted = active - centre
    spread = jnp.mean(shifted * shifted, axis=-1, keepdims=True)
    return (shifted * lax.rsqrt(spread + 1e-05)).astype(jnp.bfloat16)


def exchange_kernel(
    groups,
    shards,
    lq,
    query_ref,
    positive_ref,
    cls_ref,
    meta_ref,
    transform_ref,
    store_ref,
    vocab_ref,
    tables_out,
    cls_out,
    meta_out,
    hidden,
    vocab,
    cls_buf,
    meta_buf,
    front,
    coded,
    query_pool,
    passage_pool,
    partial,
    tables,
    load_sem,
    tree_send,
    tree_recv,
    meta_send,
    meta_recv,
    pool_send,
    pool_recv,
    part_send,
    part_recv,
    table_send,
    table_recv,
):
    group = lax.axis_index("group")
    shard = lax.axis_index("shard")
    devices = groups * shards
    linear = group * shards + shard
    bits = shards.bit_length() - 1
    queries, lp, width = positive_ref.shape
    chunks, _, chunk_rows, _ = coded.shape
    chunk_passages = chunk_rows // lp
    share = chunks * chunk_passages
    columns = vocab.shape[1]
    front_query = queries * lq
    store_total = share * shards

    digit = [(shard // (1 << i)) % 2 for i in range(bits)]

    def partner(offset):
        index = 0
        for i in range(bits):
            index = index + ((1 - digit[i]) if (offset >> i) & 1 else digit[i]) * (1 << i)
        return index

    peers = [partner(offset) for offset in range(shards)]

    load_store = pltpu.make_async_copy(
        store_ref.at[pl.ds(group * share, share)], hidden, load_sem.at[0]
    )
    load_vocab = pltpu.make_async_copy(vocab_ref, vocab, load_sem.at[1])
    load_store.start()
    load_vocab.start()

    barrier = pltpu.get_barrier_semaphore()

    def greet(i, carry):
        other = (linear + i) % devices
        pl.semaphore_signal(
            barrier, inc=1, device_id=(other // shards, other % shards), device_id_type=MESH_ID
        )
        return carry

    lax.fori_loop(1, devices, greet, 0)

    def block(chunk, slot):
        if chunk == 0:
            return cls_buf.at[slot]
        if chunk == 1:
            return front.at[slot]
        return coded.at[chunk - 2, slot]

    def order(chunk):
        outer = list(range(1, bits))
        return (outer if chunk % 2 == 0 else outer[::-1]) + [0]

    def hop(chunk, offset, dim):
        source = cls_ref if chunk == 0 and offset == 0 else block(chunk, peers[offset])
        return pltpu.make_async_remote_copy(
            src_ref=source,
            dst_ref=block(chunk, peers[offset]),
            send_sem=tree_send.at[chunk, offset, dim],
            recv_sem=tree_recv.at[chunk, offset ^ (1 << dim)],
            device_id={"shard": peers[1 << dim]},
            device_id_type=MESH_ID,
        )

    def arrived(chunk, offset):
        pltpu.make_async_remote_copy(
            src_ref=block(chunk, peers[offset]),
            dst_ref=block(chunk, peers[offset]),
            send_sem=tree_send.at[chunk, 0, 0],
            recv_sem=tree_recv.at[chunk, offset],
            device_id={"shard": peers[1]},
            device_id_type=MESH_ID,
        ).wait_recv()

    hops = []

    def forward(chunk, offset):
        path = order(chunk)
        last = max([path.index(i) for i in range(bits) if (offset >> i) & 1], default=-1)
        for dim in path[last + 1 :]:
            copy = hop(chunk, offset, dim)
            copy.start()
            hops.append(copy)

    def relay(chunk, level):
        for offset in range(0, shards, 2):
            if offset.bit_count() == level:
                arrived(chunk, offset)
                forward(chunk, offset)

    def finish(chunk):
        for offset in range(1, shards, 2):
            arrived(chunk, offset)

    def encode_chunk(chunk):
        if chunk == 1:
            rows = jnp.concatenate(
                [
                    query_ref[...].reshape(front_query, width),
                    positive_ref[...].reshape(queries * lp, width),
                ],
                axis=0,
            )
            front[shard] = encode(rows, transform_ref[...])
        else:
            first = (chunk - 2) * chunk_passages
            rows = hidden[first : first + chunk_passages].reshape(chunk_rows, width)
            coded[chunk - 2, shard] = encode(rows, transform_ref[...])

    def pool(rows, length, target):
        sequences = rows.shape[0] // length
        for start in range(0, columns, COLS):
            stop = min(start + COLS, columns)
            logits = jnp.dot(rows, vocab[:, start:stop], preferred_element_type=jnp.float32)
            best = jnp.max(logits.reshape(sequences, length, stop - start), axis=1)
            target(start, stop, jnp.log1p(jnp.maximum(best, 0.0)))

    def pool_front():
        def put_query(start, stop, values):
            query_pool[group, :, start:stop] = values

        def put_positive(start, stop, values):
            passage_pool[store_total : store_total + shards * queries, start:stop] = values

        pool(front[:, :front_query].reshape(shards * front_query, width), lq, put_query)
        for i in range(1, groups):
            send_pool(i).start()
        pool(front[:, front_query:].reshape(shards * queries * lp, width), lp, put_positive)

    slots = max(1, min(shards, TILE_ROWS // chunk_rows))

    def pool_chunk(chunk):
        def step(i, carry):
            rows = coded[chunk - 2, pl.ds(i * slots, slots)].reshape(slots * chunk_rows, width)
            tall = slots * chunk_passages
            base = (chunk - 2) * shards * chunk_passages + i * tall

            def put(start, stop, values):
                passage_pool[pl.ds(pl.multiple_of(base, tall), tall), start:stop] = values

            pool(rows, lp, put)
            return carry

        lax.fori_loop(0, shards // slots, step, 0)

    def send_pool(i):
        return pltpu.make_async_remote_copy(
            src_ref=query_pool.at[group],
            dst_ref=query_pool.at[group],
            send_sem=pool_send.at[i],
            recv_sem=pool_recv.at[i],
            device_id={"group": (group + i) % groups},
            device_id_type=MESH_ID,
        )

    def pool_arrived(i):
        slot = (group + groups - i) % groups
        pltpu.make_async_remote_copy(
            src_ref=query_pool.at[slot],
            dst_ref=query_pool.at[slot],
            send_sem=pool_send.at[i],
            recv_sem=pool_recv.at[i],
            device_id={"group": (group + i) % groups},
            device_id_type=MESH_ID,
        ).wait_recv()

    def meta_copy(i, sender):
        other = (linear + i) % devices
        return pltpu.make_async_remote_copy(
            src_ref=meta_ref,
            dst_ref=meta_buf.at[sender],
            send_sem=meta_send.at[i],
            recv_sem=meta_recv.at[i],
            device_id=(other // shards, other % shards),
            device_id_type=MESH_ID,
        )

    encode_chunk(1)
    cls_buf[shard] = cls_ref[...]
    meta_buf[linear] = meta_ref[...]
    passage_pool[store_total + shards * queries :, :] = jnp.zeros(
        (passage_pool.shape[0] - store_total - shards * queries, columns), jnp.float32
    )
    pl.semaphore_wait(barrier, devices - 1)

    total = chunks + 2
    for step in range(total + bits - 1):
        if step < total:
            if step == 2:
                load_store.wait()
            if step >= 2:
                encode_chunk(step)
            forward(step, 0)
            if step == 1:

                def send_meta(i, carry):
                    meta_copy(i, linear).start()
                    return carry

                lax.fori_loop(1, devices, send_meta, 0)
        for level in range(1, bits):
            if 0 <= step - level < total:
                relay(step - level, level)
        ready = step - bits + 1
        if 0 <= ready < total:
            finish(ready)
            if ready == 1:
                load_vocab.wait()
                pool_front()
            elif ready > 1:
                pool_chunk(ready)

    for i in range(1, groups):
        pool_arrived(i)
    stacked = query_pool[...].reshape(groups * shards * queries, columns)
    partial[shard] = lax.dot_general(
        stacked,
        passage_pool[...],
        (((1,), (1,)), ((), ())),
        precision=HIGHEST,
        preferred_element_type=jnp.float32,
    )

    def part_copy(offset, slot):
        return pltpu.make_async_remote_copy(
            src_ref=partial.at[slot],
            dst_ref=partial.at[slot],
            send_sem=part_send.at[offset],
            recv_sem=part_recv.at[offset],
            device_id={"shard": peers[offset]},
            device_id_type=MESH_ID,
        )

    for offset in range(1, shards):
        part_copy(offset, shard).start()
    for offset in range(1, shards):
        part_copy(offset, peers[offset]).wait_recv()
    tables[group] = jnp.sum(partial[...], axis=0)

    def table_copy(i, slot):
        return pltpu.make_async_remote_copy(
            src_ref=tables.at[slot],
            dst_ref=tables.at[slot],
            send_sem=table_send.at[i],
            recv_sem=table_recv.at[i],
            device_id={"group": (group + i) % groups},
            device_id_type=MESH_ID,
        )

    for i in range(1, groups):
        table_copy(i, group).start()

    def meta_arrived(i, carry):
        meta_copy(i, (linear + devices - i) % devices).wait_recv()
        return carry

    lax.fori_loop(1, devices, meta_arrived, 0)
    cls_out[...] = cls_buf[...]
    meta_out[...] = meta_buf[...]

    def meta_sent(i, carry):
        meta_copy(i, linear).wait_send()
        return carry

    lax.fori_loop(1, devices, meta_sent, 0)
    for copy in hops:
        copy.wait_send()
    for i in range(1, groups):
        send_pool(i).wait_send()
    for offset in range(1, shards):
        part_copy(offset, shard).wait_send()
    for i in range(1, groups):
        table_copy(i, (group + groups - i) % groups).wait_recv()
    tables_out[...] = tables[...]
    for i in range(1, groups):
        table_copy(i, group).wait_send()


def dot(left, right, dims):
    return lax.dot_general(
        left, right, (dims, ((), ())), precision=HIGHEST, preferred_element_type=jnp.float32
    )


def split_dot(left, right):
    high = right.astype(jnp.bfloat16)
    rest = right - high.astype(jnp.float32)
    low = rest.astype(jnp.bfloat16)
    dims = (((0,), (0,)), ((), ()))
    return lax.dot_general(
        left, high, dims, preferred_element_type=jnp.float32
    ) + lax.dot_general(left, low, dims, preferred_element_type=jnp.float32)


def loss_kernel(
    groups,
    shards,
    negatives,
    chunk_passages,
    vocab_total,
    tables_ref,
    cls_ref,
    meta_ref,
    dense_ref,
    margin_ref,
    grad_ref,
    margin_buf,
):
    _, store_rows, width = cls_ref.shape
    total, _, lanes = meta_ref.shape
    passages = shards * store_rows
    own = margin_ref.shape[0]
    share = store_rows // groups
    chunks = share // chunk_passages
    parts = width // lanes
    table_cols = tables_ref.shape[2]
    inv_root = 1.0 / math.sqrt(width)
    inv_vocab = 1.0 / math.sqrt(vocab_total)
    query_cls = jnp.concatenate([meta_ref[:, i, :] for i in range(parts)], axis=1).astype(
        jnp.bfloat16
    )
    positive_cls = jnp.concatenate(
        [meta_ref[:, parts + i, :] for i in range(parts)], axis=1
    ).astype(jnp.bfloat16)
    labels = meta_ref[:, 2 * parts, :]
    ids = labels[:, :negatives].astype(jnp.int32)
    targets = labels[:, negatives : 2 * negatives] / 1024.0
    store_cls = cls_ref[...].reshape(passages, width)
    dense = dense_ref[...]
    query_vec = jnp.dot(query_cls, dense, preferred_element_type=jnp.float32)
    positive_vec = jnp.dot(positive_cls, dense, preferred_element_type=jnp.float32)
    store_vec = jnp.dot(store_cls, dense, preferred_element_type=jnp.float32)
    dense_pos = jnp.sum(query_vec * positive_vec, axis=1, keepdims=True) * inv_root
    dense_all = dot(query_vec, store_vec, ((1,), (1,))) * inv_root

    row = lax.broadcasted_iota(jnp.int32, (total, table_cols), 0)
    column = lax.broadcasted_iota(jnp.int32, (total, table_cols), 1)
    span = total // groups
    sparse_pos = jnp.zeros((total, 1), jnp.float32)
    for g in range(groups):
        hit = (row - g * span) == (column - share * shards)
        hit = hit & (column >= share * shards) & (row >= g * span) & (row < (g + 1) * span)
        sparse_pos = sparse_pos + jnp.sum(
            jnp.where(hit, tables_ref[g], 0.0), axis=1, keepdims=True
        )
    pos_score = sparse_pos * inv_vocab + dense_pos

    passage = lax.broadcasted_iota(jnp.int32, (total, passages), 1)
    weights = jnp.zeros((total, passages), jnp.float32)
    coef_total = jnp.zeros((total, 1), jnp.float32)
    margins = jnp.zeros((total, table_cols), jnp.float32)
    for k in range(negatives):
        number = ids[:, k : k + 1]
        owner = number // store_rows
        local = number - owner * store_rows
        part = local // share
        inner = local - part * share
        chunk = inner // chunk_passages
        place = (chunk * shards + owner) * chunk_passages + inner - chunk * chunk_passages
        here = column == place
        sparse_neg = jnp.zeros((total, 1), jnp.float32)
        for g in range(groups):
            sparse_neg = sparse_neg + jnp.sum(
                jnp.where(here & (part == g), tables_ref[g], 0.0), axis=1, keepdims=True
            )
        named = passage == number
        dense_neg = jnp.sum(jnp.where(named, dense_all, 0.0), axis=1, keepdims=True)
        margin = pos_score - (sparse_neg * inv_vocab + dense_neg)
        coef = (margin - targets[:, k : k + 1]) / negatives
        weights = weights + jnp.where(named, coef, 0.0)
        coef_total = coef_total + coef
        margins = jnp.where(column == k, margin, margins)
    margin_buf[...] = margins
    linear = lax.axis_index("group") * shards + lax.axis_index("shard")
    margin_ref[...] = margin_buf[pl.ds(linear * own, own), :negatives]

    grad_query = (coef_total * positive_vec - dot(weights, store_vec, ((1,), (0,)))) * inv_root
    grad_positive = coef_total * query_vec * inv_root
    grad_store = dot(weights, query_vec, ((0,), (0,))) * (-inv_root)
    states = jnp.concatenate([query_cls, positive_cls, store_cls], axis=0)
    factors = jnp.concatenate([grad_query, grad_positive, grad_store], axis=0)
    grad_ref[...] = split_dot(states, factors)


def body(
    query_hidden,
    positive_hidden,
    passage_store,
    negative_ids,
    teacher_margins,
    transform_weight,
    vocab_weight,
    dense_weight,
):
    groups = lax.axis_size("group")
    shards = lax.axis_size("shard")
    devices = groups * shards
    bits = shards.bit_length() - 1
    queries, lq, width = query_hidden.shape
    store_rows, lp, _ = passage_store.shape
    negatives = negative_ids.shape[1]
    columns = vocab_weight.shape[1]
    share = store_rows // groups
    chunk_passages = min(CHUNK_PASSAGES, share)
    chunks = share // chunk_passages
    parts = width // LANES
    rows = 2 * parts + 1
    rows += -rows % 8
    pooled = share * shards + shards * queries
    pooled += -pooled % 128
    total = devices * queries

    labels = jnp.concatenate([negative_ids, teacher_margins], axis=1).astype(jnp.float32)
    labels = jnp.pad(labels, ((0, 0), (0, LANES - 2 * negatives)))
    meta = jnp.concatenate(
        [
            query_hidden[:, 0, :].astype(jnp.float32).reshape(queries, parts, LANES),
            positive_hidden[:, 0, :].astype(jnp.float32).reshape(queries, parts, LANES),
            labels[:, None, :],
            jnp.zeros((queries, rows - 2 * parts - 1, LANES), jnp.float32),
        ],
        axis=1,
    )
    store_cls = passage_store[:, 0, :]

    vmem = pl.BlockSpec(memory_space=pltpu.VMEM)
    hbm = pl.BlockSpec(memory_space=pl.ANY)
    dma = pltpu.SemaphoreType.DMA
    tables, cls_all, meta_all = pl.pallas_call(
        functools.partial(exchange_kernel, groups, shards, lq),
        out_shape=[
            jax.ShapeDtypeStruct((groups, total, pooled), jnp.float32),
            jax.ShapeDtypeStruct((shards, store_rows, width), jnp.bfloat16),
            jax.ShapeDtypeStruct((devices, queries, rows, LANES), jnp.float32),
        ],
        in_specs=[vmem] * 5 + [hbm] * 2,
        out_specs=[vmem] * 3,
        scratch_shapes=[
            pltpu.VMEM((share, lp, width), jnp.bfloat16),
            pltpu.VMEM((width, columns), jnp.bfloat16),
            pltpu.VMEM((shards, store_rows, width), jnp.bfloat16),
            pltpu.VMEM((devices, queries, rows, LANES), jnp.float32),
            pltpu.VMEM((shards, queries * (lq + lp), width), jnp.bfloat16),
            pltpu.VMEM((chunks, shards, chunk_passages * lp, width), jnp.bfloat16),
            pltpu.VMEM((groups, shards * queries, columns), jnp.float32),
            pltpu.VMEM((pooled, columns), jnp.float32),
            pltpu.VMEM((shards, total, pooled), jnp.float32),
            pltpu.VMEM((groups, total, pooled), jnp.float32),
            dma((2,)),
            dma((chunks + 2, shards, bits)),
            dma((chunks + 2, shards)),
            dma((devices,)),
            dma((devices,)),
            dma((groups,)),
            dma((groups,)),
            dma((shards,)),
            dma((shards,)),
            dma((groups,)),
            dma((groups,)),
        ],
        compiler_params=pltpu.CompilerParams(
            collective_id=0, has_side_effects=True, vmem_limit_bytes=56 * 1024 * 1024
        ),
        name="exchange",
    )(
        query_hidden,
        positive_hidden,
        store_cls,
        meta,
        transform_weight,
        passage_store,
        vocab_weight,
    )
    return pl.pallas_call(
        functools.partial(
            loss_kernel, groups, shards, negatives, chunk_passages, columns * shards
        ),
        out_shape=[
            jax.ShapeDtypeStruct((queries, negatives), jnp.float32),
            jax.ShapeDtypeStruct((width, width), jnp.float32),
        ],
        in_specs=[vmem] * 4,
        out_specs=[vmem] * 2,
        scratch_shapes=[pltpu.VMEM((total, pooled), jnp.float32)],
        compiler_params=pltpu.CompilerParams(vmem_limit_bytes=32 * 1024 * 1024),
        name="loss",
    )(tables, cls_all, meta_all.reshape(total, rows, LANES), dense_weight)


def solution(mesh):
    in_specs = (
        P(("group", "shard"), None, None),
        P(("group", "shard"), None, None),
        P("shard", None, None),
        P(("group", "shard"), None),
        P(("group", "shard"), None),
        P(),
        P(None, "shard"),
        P(),
    )
    out_specs = (P(("group", "shard"), None), P())
    return jax.shard_map(body, mesh=mesh, in_specs=in_specs, out_specs=out_specs, check_vma=False)
```

```python
import functools
import math

import jax
import jax.numpy as jnp
from jax import lax
from jax.experimental import pallas as pl
from jax.experimental.pallas import tpu as pltpu
from jax.sharding import PartitionSpec as P

LANES = 256
COLS = 512
TILE_ROWS = 512
CHUNK_PASSAGES = 2
HIGHEST = lax.Precision.HIGHEST
MESH_ID = pl.DeviceIdType.MESH


def encode(hidden, transform_weight):
    mixed = jnp.dot(hidden, transform_weight, preferred_element_type=jnp.float32)
    active = 0.5 * mixed * (1.0 + lax.erf(mixed * math.sqrt(0.5)))
    centre = jnp.mean(active, axis=-1, keepdims=True)
    shifted = active - centre
    spread = jnp.mean(shifted * shifted, axis=-1, keepdims=True)
    return (shifted * lax.rsqrt(spread + 1e-05)).astype(jnp.bfloat16)


def exchange_kernel(
    groups,
    shards,
    lq,
    query_ref,
    positive_ref,
    ids_ref,
    teacher_ref,
    transform_ref,
    store_ref,
    vocab_ref,
    tables_out,
    cls_out,
    meta_out,
    heads,
    hidden,
    vocab,
    cls_buf,
    meta_buf,
    front,
    coded,
    query_pool,
    passage_pool,
    partial,
    tables,
    load_sem,
    tree_send,
    tree_recv,
    meta_send,
    meta_recv,
    pool_send,
    pool_recv,
    part_send,
    part_recv,
    table_send,
    table_recv,
):
    group = lax.axis_index("group")
    shard = lax.axis_index("shard")
    devices = groups * shards
    linear = group * shards + shard
    bits = shards.bit_length() - 1
    queries, lp, width = positive_ref.shape
    chunks, _, chunk_rows, _ = coded.shape
    chunk_passages = chunk_rows // lp
    share = chunks * chunk_passages
    columns = vocab.shape[1]
    front_query = queries * lq
    store_total = share * shards

    digit = [(shard // (1 << i)) % 2 for i in range(bits)]

    def partner(offset):
        index = 0
        for i in range(bits):
            index = index + ((1 - digit[i]) if (offset >> i) & 1 else digit[i]) * (1 << i)
        return index

    peers = [partner(offset) for offset in range(shards)]

    load_store = pltpu.make_async_copy(
        store_ref.at[pl.ds(group * share, share)], hidden, load_sem.at[0]
    )
    load_vocab = pltpu.make_async_copy(vocab_ref, vocab, load_sem.at[1])
    load_heads = pltpu.make_async_copy(
        store_ref.at[:, pl.ds(0, heads.shape[1])], heads, load_sem.at[2]
    )
    load_heads.start()
    load_store.start()
    load_vocab.start()

    barrier = pltpu.get_barrier_semaphore()

    def greet(i, carry):
        other = (linear + i) % devices
        pl.semaphore_signal(
            barrier, inc=1, device_id=(other // shards, other % shards), device_id_type=MESH_ID
        )
        return carry

    lax.fori_loop(1, devices, greet, 0)

    def block(chunk, half, slot):
        if chunk == 0:
            ref = front.at[slot]
        elif chunk == 1:
            ref = cls_buf.at[slot]
        else:
            ref = coded.at[chunk - 2, slot]
        rows = ref.shape[0] // 2
        return ref.at[pl.ds(half * rows, rows)]

    def order(half):
        outer = list(range(1, bits))
        return (outer if half == 0 else outer[::-1]) + [0]

    def hop(chunk, half, offset, dim):
        piece = block(chunk, half, peers[offset])
        return pltpu.make_async_remote_copy(
            src_ref=piece,
            dst_ref=piece,
            send_sem=tree_send.at[2 * chunk + half, offset, dim],
            recv_sem=tree_recv.at[2 * chunk + half, offset ^ (1 << dim)],
            device_id={"shard": peers[1 << dim]},
            device_id_type=MESH_ID,
        )

    def arrived(chunk, half, offset):
        piece = block(chunk, half, peers[offset])
        pltpu.make_async_remote_copy(
            src_ref=piece,
            dst_ref=piece,
            send_sem=tree_send.at[2 * chunk + half, 0, 0],
            recv_sem=tree_recv.at[2 * chunk + half, offset],
            device_id={"shard": peers[1]},
            device_id_type=MESH_ID,
        ).wait_recv()

    hops = []

    def forward(chunk, half, offset):
        path = order(half)
        last = max([path.index(i) for i in range(bits) if (offset >> i) & 1], default=-1)
        for dim in path[last + 1 :]:
            copy = hop(chunk, half, offset, dim)
            copy.start()
            hops.append(copy)

    def relay(chunk, level):
        for offset in range(0, shards, 2):
            if offset.bit_count() == level:
                for half in range(2):
                    arrived(chunk, half, offset)
                    forward(chunk, half, offset)

    def finish(chunk):
        for offset in range(1, shards, 2):
            for half in range(2):
                arrived(chunk, half, offset)

    def first_token(values):
        values = values.astype(jnp.float32)
        token = lax.broadcasted_iota(jnp.int32, values.shape, 1)
        return jnp.sum(jnp.where(token == 0, values, 0.0), axis=1)

    def encode_chunk(chunk):
        if chunk == 0:
            rows = jnp.concatenate(
                [
                    query_ref[...].reshape(front_query, width),
                    positive_ref[...].reshape(queries * lp, width),
                ],
                axis=0,
            )
            front[shard] = encode(rows, transform_ref[...])
        elif chunk == 1:
            load_heads.wait()
            cls_buf[shard] = first_token(heads[...]).astype(jnp.bfloat16)
            meta_buf[linear] = jnp.zeros(meta_buf.shape[1:], jnp.float32)
            parts = width // LANES
            for i, ref in enumerate((query_ref, positive_ref)):
                states = first_token(ref[:, :8])
                for j in range(parts):
                    meta_buf[linear, :, i * parts + j, :] = states[:, j * LANES : (j + 1) * LANES]
            negatives = ids_ref.shape[1]
            meta_buf[linear, :, 2 * parts, :negatives] = ids_ref[...].astype(jnp.float32)
            meta_buf[linear, :, 2 * parts, negatives : 2 * negatives] = teacher_ref[
                ...
            ].astype(jnp.float32)
        else:
            first = (chunk - 2) * chunk_passages
            rows = hidden[first : first + chunk_passages].reshape(chunk_rows, width)
            coded[chunk - 2, shard] = encode(rows, transform_ref[...])

    def pool(rows, length, target):
        sequences = rows.shape[0] // length
        for start in range(0, columns, COLS):
            stop = min(start + COLS, columns)
            logits = jnp.dot(rows, vocab[:, start:stop], preferred_element_type=jnp.float32)
            best = jnp.max(logits.reshape(sequences, length, stop - start), axis=1)
            target(start, stop, jnp.log1p(jnp.maximum(best, 0.0)))

    def pool_front():
        def put_query(start, stop, values):
            query_pool[group, :, start:stop] = values

        def put_positive(start, stop, values):
            passage_pool[store_total : store_total + shards * queries, start:stop] = values

        pool(front[:, :front_query].reshape(shards * front_query, width), lq, put_query)
        for i in range(1, groups):
            send_pool(i).start()
        pool(front[:, front_query:].reshape(shards * queries * lp, width), lp, put_positive)

    slots = max(1, min(shards, TILE_ROWS // chunk_rows))

    def pool_chunk(chunk):
        def step(i, carry):
            rows = coded[chunk - 2, pl.ds(i * slots, slots)].reshape(slots * chunk_rows, width)
            tall = slots * chunk_passages
            base = (chunk - 2) * shards * chunk_passages + i * tall

            def put(start, stop, values):
                passage_pool[pl.ds(pl.multiple_of(base, tall), tall), start:stop] = values

            pool(rows, lp, put)
            return carry

        lax.fori_loop(0, shards // slots, step, 0)

    def send_pool(i):
        return pltpu.make_async_remote_copy(
            src_ref=query_pool.at[group],
            dst_ref=query_pool.at[group],
            send_sem=pool_send.at[i],
            recv_sem=pool_recv.at[i],
            device_id={"group": (group + i) % groups},
            device_id_type=MESH_ID,
        )

    def pool_arrived(i):
        slot = (group + groups - i) % groups
        pltpu.make_async_remote_copy(
            src_ref=query_pool.at[slot],
            dst_ref=query_pool.at[slot],
            send_sem=pool_send.at[i],
            recv_sem=pool_recv.at[i],
            device_id={"group": (group + i) % groups},
            device_id_type=MESH_ID,
        ).wait_recv()

    def meta_copy(i, sender):
        other = (linear + i) % devices
        return pltpu.make_async_remote_copy(
            src_ref=meta_buf.at[sender],
            dst_ref=meta_buf.at[sender],
            send_sem=meta_send.at[i],
            recv_sem=meta_recv.at[i],
            device_id=(other // shards, other % shards),
            device_id_type=MESH_ID,
        )

    encode_chunk(0)
    encode_chunk(1)
    passage_pool[store_total + shards * queries :, :] = jnp.zeros(
        (passage_pool.shape[0] - store_total - shards * queries, columns), jnp.float32
    )
    pl.semaphore_wait(barrier, devices - 1)

    total = chunks + 2
    for step in range(total + bits - 1):
        if step < total:
            if step == 2:
                load_store.wait()
            if step >= 2:
                encode_chunk(step)
            forward(step, 0, 0)
            forward(step, 1, 0)
            if step == 1:

                def send_meta(i, carry):
                    meta_copy(i, linear).start()
                    return carry

                lax.fori_loop(1, devices, send_meta, 0)
        for level in range(1, bits):
            if 0 <= step - level < total:
                relay(step - level, level)
        ready = step - bits + 1
        if 0 <= ready < total:
            finish(ready)
            if ready == 0:
                load_vocab.wait()
                pool_front()
            elif ready > 1:
                pool_chunk(ready)

    for i in range(1, groups):
        pool_arrived(i)
    stacked = query_pool[...].reshape(groups * shards * queries, columns)
    partial[shard] = lax.dot_general(
        stacked,
        passage_pool[...],
        (((1,), (1,)), ((), ())),
        precision=HIGHEST,
        preferred_element_type=jnp.float32,
    )

    def part_copy(offset, slot):
        return pltpu.make_async_remote_copy(
            src_ref=partial.at[slot],
            dst_ref=partial.at[slot],
            send_sem=part_send.at[offset],
            recv_sem=part_recv.at[offset],
            device_id={"shard": peers[offset]},
            device_id_type=MESH_ID,
        )

    for offset in range(1, shards):
        part_copy(offset, shard).start()
    for offset in range(1, shards):
        part_copy(offset, peers[offset]).wait_recv()
    tables[group] = jnp.sum(partial[...], axis=0)

    def table_copy(i, slot):
        return pltpu.make_async_remote_copy(
            src_ref=tables.at[slot],
            dst_ref=tables.at[slot],
            send_sem=table_send.at[i],
            recv_sem=table_recv.at[i],
            device_id={"group": (group + i) % groups},
            device_id_type=MESH_ID,
        )

    for i in range(1, groups):
        table_copy(i, group).start()

    def meta_arrived(i, carry):
        meta_copy(i, (linear + devices - i) % devices).wait_recv()
        return carry

    lax.fori_loop(1, devices, meta_arrived, 0)
    cls_out[...] = cls_buf[...]
    meta_out[...] = meta_buf[...]

    def meta_sent(i, carry):
        meta_copy(i, linear).wait_send()
        return carry

    lax.fori_loop(1, devices, meta_sent, 0)
    for copy in hops:
        copy.wait_send()
    for i in range(1, groups):
        send_pool(i).wait_send()
    for offset in range(1, shards):
        part_copy(offset, shard).wait_send()
    for i in range(1, groups):
        table_copy(i, (group + groups - i) % groups).wait_recv()
    tables_out[...] = tables[...]
    for i in range(1, groups):
        table_copy(i, group).wait_send()


def dot(left, right, dims):
    return lax.dot_general(
        left, right, (dims, ((), ())), precision=HIGHEST, preferred_element_type=jnp.float32
    )


def split_dot(left, right):
    high = right.astype(jnp.bfloat16)
    rest = right - high.astype(jnp.float32)
    low = rest.astype(jnp.bfloat16)
    dims = (((0,), (0,)), ((), ()))
    return lax.dot_general(
        left, high, dims, preferred_element_type=jnp.float32
    ) + lax.dot_general(left, low, dims, preferred_element_type=jnp.float32)


def loss_kernel(
    groups,
    shards,
    negatives,
    chunk_passages,
    vocab_total,
    tables_ref,
    cls_ref,
    meta_ref,
    dense_ref,
    margin_ref,
    grad_ref,
    margin_buf,
):
    _, store_rows, width = cls_ref.shape
    total, _, lanes = meta_ref.shape
    passages = shards * store_rows
    own = margin_ref.shape[0]
    share = store_rows // groups
    chunks = share // chunk_passages
    parts = width // lanes
    table_cols = tables_ref.shape[2]
    inv_root = 1.0 / math.sqrt(width)
    inv_vocab = 1.0 / math.sqrt(vocab_total)
    query_cls = jnp.concatenate([meta_ref[:, i, :] for i in range(parts)], axis=1).astype(
        jnp.bfloat16
    )
    positive_cls = jnp.concatenate(
        [meta_ref[:, parts + i, :] for i in range(parts)], axis=1
    ).astype(jnp.bfloat16)
    labels = meta_ref[:, 2 * parts, :]
    ids = labels[:, :negatives].astype(jnp.int32)
    targets = labels[:, negatives : 2 * negatives] / 1024.0
    store_cls = cls_ref[...].reshape(passages, width)
    dense = dense_ref[...]
    query_vec = jnp.dot(query_cls, dense, preferred_element_type=jnp.float32)
    positive_vec = jnp.dot(positive_cls, dense, preferred_element_type=jnp.float32)
    store_vec = jnp.dot(store_cls, dense, preferred_element_type=jnp.float32)
    dense_pos = jnp.sum(query_vec * positive_vec, axis=1, keepdims=True) * inv_root
    dense_all = dot(query_vec, store_vec, ((1,), (1,))) * inv_root

    row = lax.broadcasted_iota(jnp.int32, (total, table_cols), 0)
    column = lax.broadcasted_iota(jnp.int32, (total, table_cols), 1)
    span = total // groups
    sparse_pos = jnp.zeros((total, 1), jnp.float32)
    for g in range(groups):
        hit = (row - g * span) == (column - share * shards)
        hit = hit & (column >= share * shards) & (row >= g * span) & (row < (g + 1) * span)
        sparse_pos = sparse_pos + jnp.sum(
            jnp.where(hit, tables_ref[g], 0.0), axis=1, keepdims=True
        )
    pos_score = sparse_pos * inv_vocab + dense_pos

    passage = lax.broadcasted_iota(jnp.int32, (total, passages), 1)
    weights = jnp.zeros((total, passages), jnp.float32)
    coef_total = jnp.zeros((total, 1), jnp.float32)
    margins = jnp.zeros((total, table_cols), jnp.float32)
    for k in range(negatives):
        number = ids[:, k : k + 1]
        owner = number // store_rows
        local = number - owner * store_rows
        part = local // share
        inner = local - part * share
        chunk = inner // chunk_passages
        place = (chunk * shards + owner) * chunk_passages + inner - chunk * chunk_passages
        here = column == place
        sparse_neg = jnp.zeros((total, 1), jnp.float32)
        for g in range(groups):
            sparse_neg = sparse_neg + jnp.sum(
                jnp.where(here & (part == g), tables_ref[g], 0.0), axis=1, keepdims=True
            )
        named = passage == number
        dense_neg = jnp.sum(jnp.where(named, dense_all, 0.0), axis=1, keepdims=True)
        margin = pos_score - (sparse_neg * inv_vocab + dense_neg)
        coef = (margin - targets[:, k : k + 1]) / negatives
        weights = weights + jnp.where(named, coef, 0.0)
        coef_total = coef_total + coef
        margins = jnp.where(column == k, margin, margins)
    margin_buf[...] = margins
    linear = lax.axis_index("group") * shards + lax.axis_index("shard")
    margin_ref[...] = margin_buf[pl.ds(linear * own, own), :negatives]

    grad_query = (coef_total * positive_vec - dot(weights, store_vec, ((1,), (0,)))) * inv_root
    grad_positive = coef_total * query_vec * inv_root
    grad_store = dot(weights, query_vec, ((0,), (0,))) * (-inv_root)
    states = jnp.concatenate([query_cls, positive_cls, store_cls], axis=0)
    factors = jnp.concatenate([grad_query, grad_positive, grad_store], axis=0)
    grad_ref[...] = split_dot(states, factors)


def body(
    query_hidden,
    positive_hidden,
    passage_store,
    negative_ids,
    teacher_margins,
    transform_weight,
    vocab_weight,
    dense_weight,
):
    groups = lax.axis_size("group")
    shards = lax.axis_size("shard")
    devices = groups * shards
    bits = shards.bit_length() - 1
    queries, lq, width = query_hidden.shape
    store_rows, lp, _ = passage_store.shape
    negatives = negative_ids.shape[1]
    columns = vocab_weight.shape[1]
    share = store_rows // groups
    chunk_passages = min(CHUNK_PASSAGES, share)
    chunks = share // chunk_passages
    rows = 2 * (width // LANES) + 1
    rows += -rows % 8
    pooled = share * shards + shards * queries
    pooled += -pooled % 128
    total = devices * queries

    vmem = pl.BlockSpec(memory_space=pltpu.VMEM)
    hbm = pl.BlockSpec(memory_space=pl.ANY)
    dma = pltpu.SemaphoreType.DMA
    tables, cls_all, meta_all = pl.pallas_call(
        functools.partial(exchange_kernel, groups, shards, lq),
        out_shape=[
            jax.ShapeDtypeStruct((groups, total, pooled), jnp.float32),
            jax.ShapeDtypeStruct((shards, store_rows, width), jnp.bfloat16),
            jax.ShapeDtypeStruct((devices, queries, rows, LANES), jnp.float32),
        ],
        in_specs=[vmem] * 5 + [hbm] * 2,
        out_specs=[vmem] * 3,
        scratch_shapes=[
            pltpu.VMEM((store_rows, 8, width), jnp.bfloat16),
            pltpu.VMEM((share, lp, width), jnp.bfloat16),
            pltpu.VMEM((width, columns), jnp.bfloat16),
            pltpu.VMEM((shards, store_rows, width), jnp.bfloat16),
            pltpu.VMEM((devices, queries, rows, LANES), jnp.float32),
            pltpu.VMEM((shards, queries * (lq + lp), width), jnp.bfloat16),
            pltpu.VMEM((chunks, shards, chunk_passages * lp, width), jnp.bfloat16),
            pltpu.VMEM((groups, shards * queries, columns), jnp.float32),
            pltpu.VMEM((pooled, columns), jnp.float32),
            pltpu.VMEM((shards, total, pooled), jnp.float32),
            pltpu.VMEM((groups, total, pooled), jnp.float32),
            dma((3,)),
            dma((2 * (chunks + 2), shards, bits)),
            dma((2 * (chunks + 2), shards)),
            dma((devices,)),
            dma((devices,)),
            dma((groups,)),
            dma((groups,)),
            dma((shards,)),
            dma((shards,)),
            dma((groups,)),
            dma((groups,)),
        ],
        compiler_params=pltpu.CompilerParams(
            collective_id=0, has_side_effects=True, vmem_limit_bytes=56 * 1024 * 1024
        ),
        name="exchange",
    )(
        query_hidden,
        positive_hidden,
        negative_ids,
        teacher_margins,
        transform_weight,
        passage_store,
        vocab_weight,
    )
    return pl.pallas_call(
        functools.partial(
            loss_kernel, groups, shards, negatives, chunk_passages, columns * shards
        ),
        out_shape=[
            jax.ShapeDtypeStruct((queries, negatives), jnp.float32),
            jax.ShapeDtypeStruct((width, width), jnp.float32),
        ],
        in_specs=[vmem] * 4,
        out_specs=[vmem] * 2,
        scratch_shapes=[pltpu.VMEM((total, pooled), jnp.float32)],
        compiler_params=pltpu.CompilerParams(vmem_limit_bytes=32 * 1024 * 1024),
        name="loss",
    )(tables, cls_all, meta_all.reshape(total, rows, LANES), dense_weight)


def solution(mesh):
    in_specs = (
        P(("group", "shard"), None, None),
        P(("group", "shard"), None, None),
        P("shard", None, None),
        P(("group", "shard"), None),
        P(("group", "shard"), None),
        P(),
        P(None, "shard"),
        P(),
    )
    out_specs = (P(("group", "shard"), None), P())
    return jax.shard_map(body, mesh=mesh, in_specs=in_specs, out_specs=out_specs, check_vma=False)
```

```python
import functools
import math

import jax
import jax.numpy as jnp
from jax import lax
from jax.experimental import pallas as pl
from jax.experimental.pallas import tpu as pltpu
from jax.sharding import PartitionSpec as P

LANES = 256
COLS = 512
TILE_ROWS = 512
CHUNK_PASSAGES = 2
HIGHEST = lax.Precision.HIGHEST
MESH_ID = pl.DeviceIdType.MESH


def encode(hidden, transform_weight):
    mixed = jnp.dot(hidden, transform_weight, preferred_element_type=jnp.float32)
    active = 0.5 * mixed * (1.0 + lax.erf(mixed * math.sqrt(0.5)))
    centre = jnp.mean(active, axis=-1, keepdims=True)
    shifted = active - centre
    spread = jnp.mean(shifted * shifted, axis=-1, keepdims=True)
    return (shifted * lax.rsqrt(spread + 1e-05)).astype(jnp.bfloat16)


def exchange_kernel(
    groups,
    shards,
    lq,
    query_ref,
    positive_ref,
    ids_ref,
    teacher_ref,
    transform_ref,
    store_ref,
    vocab_ref,
    tables_out,
    cls_out,
    meta_out,
    heads,
    hidden,
    vocab,
    cls_buf,
    meta_buf,
    front,
    coded,
    query_pool,
    passage_pool,
    partial,
    tables,
    load_sem,
    tree_send,
    tree_recv,
    meta_send,
    meta_recv,
    pool_send,
    pool_recv,
    part_send,
    part_recv,
    table_send,
    table_recv,
):
    group = lax.axis_index("group")
    shard = lax.axis_index("shard")
    devices = groups * shards
    linear = group * shards + shard
    bits = shards.bit_length() - 1
    queries, lp, width = positive_ref.shape
    chunks, _, chunk_rows, _ = coded.shape
    chunk_passages = chunk_rows // lp
    share = chunks * chunk_passages
    columns = vocab.shape[1]
    front_query = queries * lq
    store_total = share * shards

    digit = [(shard // (1 << i)) % 2 for i in range(bits)]

    def partner(offset):
        index = 0
        for i in range(bits):
            index = index + ((1 - digit[i]) if (offset >> i) & 1 else digit[i]) * (1 << i)
        return index

    peers = [partner(offset) for offset in range(shards)]

    load_store = pltpu.make_async_copy(
        store_ref.at[pl.ds(group * share, share)], hidden, load_sem.at[0]
    )
    load_vocab = pltpu.make_async_copy(vocab_ref, vocab, load_sem.at[1])
    load_heads = pltpu.make_async_copy(
        store_ref.at[:, pl.ds(0, heads.shape[1])], heads, load_sem.at[2]
    )
    load_heads.start()
    load_store.start()
    load_vocab.start()

    barrier = pltpu.get_barrier_semaphore()

    def greet(i, carry):
        other = (linear + i) % devices
        pl.semaphore_signal(
            barrier, inc=1, device_id=(other // shards, other % shards), device_id_type=MESH_ID
        )
        return carry

    lax.fori_loop(1, devices, greet, 0)

    def block(chunk, half, slot):
        if chunk == 0:
            ref = front.at[slot]
        elif chunk == 1:
            ref = cls_buf.at[slot]
        else:
            ref = coded.at[chunk - 2, slot]
        rows = ref.shape[0] // 2
        return ref.at[pl.ds(half * rows, rows)]

    def order(half):
        outer = list(range(1, bits))
        return (outer if half == 0 else outer[::-1]) + [0]

    def hop(chunk, half, offset, dim):
        piece = block(chunk, half, peers[offset])
        return pltpu.make_async_remote_copy(
            src_ref=piece,
            dst_ref=piece,
            send_sem=tree_send.at[2 * chunk + half, offset, dim],
            recv_sem=tree_recv.at[2 * chunk + half, offset ^ (1 << dim)],
            device_id={"shard": peers[1 << dim]},
            device_id_type=MESH_ID,
        )

    def arrived(chunk, half, offset):
        piece = block(chunk, half, peers[offset])
        pltpu.make_async_remote_copy(
            src_ref=piece,
            dst_ref=piece,
            send_sem=tree_send.at[2 * chunk + half, 0, 0],
            recv_sem=tree_recv.at[2 * chunk + half, offset],
            device_id={"shard": peers[1]},
            device_id_type=MESH_ID,
        ).wait_recv()

    hops = []

    def forward(chunk, half, offset):
        path = order(half)
        last = max([path.index(i) for i in range(bits) if (offset >> i) & 1], default=-1)
        for dim in path[last + 1 :]:
            copy = hop(chunk, half, offset, dim)
            copy.start()
            hops.append(copy)

    def relay(chunk, level):
        for offset in range(0, shards, 2):
            if offset.bit_count() == level:
                for half in range(2):
                    arrived(chunk, half, offset)
                    forward(chunk, half, offset)

    def finish(chunk):
        for offset in range(1, shards, 2):
            for half in range(2):
                arrived(chunk, half, offset)

    def first_token(values):
        values = values.astype(jnp.float32)
        token = lax.broadcasted_iota(jnp.int32, values.shape, 1)
        return jnp.sum(jnp.where(token == 0, values, 0.0), axis=1)

    def encode_chunk(chunk):
        if chunk == 0:
            rows = jnp.concatenate(
                [
                    query_ref[...].reshape(front_query, width),
                    positive_ref[...].reshape(queries * lp, width),
                ],
                axis=0,
            )
            front[shard] = encode(rows, transform_ref[...])
        elif chunk == 1:
            load_heads.wait()
            cls_buf[shard] = first_token(heads[...]).astype(jnp.bfloat16)
            meta_buf[linear] = jnp.zeros(meta_buf.shape[1:], jnp.float32)
            parts = width // LANES
            for i, ref in enumerate((query_ref, positive_ref)):
                states = first_token(ref[:, :8])
                for j in range(parts):
                    meta_buf[linear, :, i * parts + j, :] = states[:, j * LANES : (j + 1) * LANES]
            negatives = ids_ref.shape[1]
            meta_buf[linear, :, 2 * parts, :negatives] = ids_ref[...].astype(jnp.float32)
            meta_buf[linear, :, 2 * parts, negatives : 2 * negatives] = teacher_ref[
                ...
            ].astype(jnp.float32)
        else:
            first = (chunk - 2) * chunk_passages
            rows = hidden[first : first + chunk_passages].reshape(chunk_rows, width)
            coded[chunk - 2, shard] = encode(rows, transform_ref[...])

    def pool(rows, length, target):
        sequences = rows.shape[0] // length
        for start in range(0, columns, COLS):
            stop = min(start + COLS, columns)
            logits = jnp.dot(rows, vocab[:, start:stop], preferred_element_type=jnp.float32)
            best = jnp.max(logits.reshape(sequences, length, stop - start), axis=1)
            target(start, stop, jnp.log1p(jnp.maximum(best, 0.0)))

    def pool_front():
        def put_query(start, stop, values):
            query_pool[group, :, start:stop] = values

        def put_positive(start, stop, values):
            passage_pool[store_total : store_total + shards * queries, start:stop] = values

        pool(front[:, :front_query].reshape(shards * front_query, width), lq, put_query)
        for i in range(1, groups):
            send_pool(i).start()
        pool(front[:, front_query:].reshape(shards * queries * lp, width), lp, put_positive)

    slots = max(1, min(shards, TILE_ROWS // chunk_rows))

    def pool_chunk(chunk):
        def step(i, carry):
            rows = coded[chunk - 2, pl.ds(i * slots, slots)].reshape(slots * chunk_rows, width)
            tall = slots * chunk_passages
            base = (chunk - 2) * shards * chunk_passages + i * tall

            def put(start, stop, values):
                passage_pool[pl.ds(pl.multiple_of(base, tall), tall), start:stop] = values

            pool(rows, lp, put)
            return carry

        lax.fori_loop(0, shards // slots, step, 0)

    def send_pool(i):
        return pltpu.make_async_remote_copy(
            src_ref=query_pool.at[group],
            dst_ref=query_pool.at[group],
            send_sem=pool_send.at[i],
            recv_sem=pool_recv.at[i],
            device_id={"group": (group + i) % groups},
            device_id_type=MESH_ID,
        )

    def pool_arrived(i):
        slot = (group + groups - i) % groups
        pltpu.make_async_remote_copy(
            src_ref=query_pool.at[slot],
            dst_ref=query_pool.at[slot],
            send_sem=pool_send.at[i],
            recv_sem=pool_recv.at[i],
            device_id={"group": (group + i) % groups},
            device_id_type=MESH_ID,
        ).wait_recv()

    def meta_copy(i, sender):
        other = (linear + i) % devices
        return pltpu.make_async_remote_copy(
            src_ref=meta_buf.at[sender],
            dst_ref=meta_buf.at[sender],
            send_sem=meta_send.at[i],
            recv_sem=meta_recv.at[i],
            device_id=(other // shards, other % shards),
            device_id_type=MESH_ID,
        )

    encode_chunk(0)
    encode_chunk(1)
    passage_pool[store_total + shards * queries :, :] = jnp.zeros(
        (passage_pool.shape[0] - store_total - shards * queries, columns), jnp.float32
    )
    pl.semaphore_wait(barrier, devices - 1)

    total = chunks + 2
    for step in range(total + bits - 1):
        if step < total:
            if step == 2:
                load_store.wait()
            if step >= 2:
                encode_chunk(step)
            forward(step, 0, 0)
            forward(step, 1, 0)
            if step == 1:

                def send_meta(i, carry):
                    meta_copy(i, linear).start()
                    return carry

                lax.fori_loop(1, devices, send_meta, 0)
        for level in range(1, bits):
            if 0 <= step - level < total:
                relay(step - level, level)
        ready = step - bits + 1
        if 0 <= ready < total:
            finish(ready)
            if ready == 0:
                load_vocab.wait()
                pool_front()
            elif ready > 1:
                pool_chunk(ready)

    for i in range(1, groups):
        pool_arrived(i)
    stacked = query_pool[...].reshape(groups * shards * queries, columns)
    partial[shard] = lax.dot_general(
        stacked,
        passage_pool[...],
        (((1,), (1,)), ((), ())),
        precision=HIGHEST,
        preferred_element_type=jnp.float32,
    )

    def part_copy(offset, slot):
        return pltpu.make_async_remote_copy(
            src_ref=partial.at[slot],
            dst_ref=partial.at[slot],
            send_sem=part_send.at[offset],
            recv_sem=part_recv.at[offset],
            device_id={"shard": peers[offset]},
            device_id_type=MESH_ID,
        )

    for offset in range(1, shards):
        part_copy(offset, shard).start()
    for offset in range(1, shards):
        part_copy(offset, peers[offset]).wait_recv()
    tables[group] = jnp.sum(partial[...], axis=0)

    def table_copy(i, slot):
        return pltpu.make_async_remote_copy(
            src_ref=tables.at[slot],
            dst_ref=tables.at[slot],
            send_sem=table_send.at[i],
            recv_sem=table_recv.at[i],
            device_id={"group": (group + i) % groups},
            device_id_type=MESH_ID,
        )

    for i in range(1, groups):
        table_copy(i, group).start()

    def meta_arrived(i, carry):
        meta_copy(i, (linear + devices - i) % devices).wait_recv()
        return carry

    lax.fori_loop(1, devices, meta_arrived, 0)
    cls_out[...] = cls_buf[...]
    meta_out[...] = meta_buf[...]

    def meta_sent(i, carry):
        meta_copy(i, linear).wait_send()
        return carry

    lax.fori_loop(1, devices, meta_sent, 0)
    for copy in hops:
        copy.wait_send()
    for i in range(1, groups):
        send_pool(i).wait_send()
    for offset in range(1, shards):
        part_copy(offset, shard).wait_send()
    for i in range(1, groups):
        table_copy(i, (group + groups - i) % groups).wait_recv()
    tables_out[...] = tables[...]
    for i in range(1, groups):
        table_copy(i, group).wait_send()


def dot(left, right, dims):
    return lax.dot_general(
        left, right, (dims, ((), ())), precision=HIGHEST, preferred_element_type=jnp.float32
    )


def split_dot(left, right):
    high = right.astype(jnp.bfloat16)
    rest = right - high.astype(jnp.float32)
    low = rest.astype(jnp.bfloat16)
    dims = (((0,), (0,)), ((), ()))
    return lax.dot_general(
        left, high, dims, preferred_element_type=jnp.float32
    ) + lax.dot_general(left, low, dims, preferred_element_type=jnp.float32)


def loss_kernel(
    groups,
    shards,
    negatives,
    chunk_passages,
    vocab_total,
    tables_hbm,
    cls_hbm,
    meta_hbm,
    dense_hbm,
    margin_ref,
    grad_ref,
    margin_buf,
    tables_ref,
    cls_ref,
    meta_ref,
    dense_ref,
    load_sem,
):
    pairs = (
        (dense_hbm, dense_ref),
        (cls_hbm, cls_ref),
        (meta_hbm, meta_ref),
        (tables_hbm, tables_ref),
    )
    loads = [
        pltpu.make_async_copy(source, target, load_sem.at[i])
        for i, (source, target) in enumerate(pairs)
    ]
    for load in loads:
        load.start()
    for load in loads:
        load.wait()
    _, store_rows, width = cls_ref.shape
    total, _, lanes = meta_ref.shape
    passages = shards * store_rows
    own = margin_ref.shape[0]
    share = store_rows // groups
    chunks = share // chunk_passages
    parts = width // lanes
    table_cols = tables_ref.shape[2]
    inv_root = 1.0 / math.sqrt(width)
    inv_vocab = 1.0 / math.sqrt(vocab_total)
    query_cls = jnp.concatenate([meta_ref[:, i, :] for i in range(parts)], axis=1).astype(
        jnp.bfloat16
    )
    positive_cls = jnp.concatenate(
        [meta_ref[:, parts + i, :] for i in range(parts)], axis=1
    ).astype(jnp.bfloat16)
    labels = meta_ref[:, 2 * parts, :]
    ids = labels[:, :negatives].astype(jnp.int32)
    targets = labels[:, negatives : 2 * negatives] / 1024.0
    store_cls = cls_ref[...].reshape(passages, width)
    dense = dense_ref[...]
    query_vec = jnp.dot(query_cls, dense, preferred_element_type=jnp.float32)
    positive_vec = jnp.dot(positive_cls, dense, preferred_element_type=jnp.float32)
    store_vec = jnp.dot(store_cls, dense, preferred_element_type=jnp.float32)
    dense_pos = jnp.sum(query_vec * positive_vec, axis=1, keepdims=True) * inv_root
    dense_all = dot(query_vec, store_vec, ((1,), (1,))) * inv_root

    row = lax.broadcasted_iota(jnp.int32, (total, table_cols), 0)
    column = lax.broadcasted_iota(jnp.int32, (total, table_cols), 1)
    span = total // groups
    sparse_pos = jnp.zeros((total, 1), jnp.float32)
    for g in range(groups):
        hit = (row - g * span) == (column - share * shards)
        hit = hit & (column >= share * shards) & (row >= g * span) & (row < (g + 1) * span)
        sparse_pos = sparse_pos + jnp.sum(
            jnp.where(hit, tables_ref[g], 0.0), axis=1, keepdims=True
        )
    pos_score = sparse_pos * inv_vocab + dense_pos

    passage = lax.broadcasted_iota(jnp.int32, (total, passages), 1)
    weights = jnp.zeros((total, passages), jnp.float32)
    coef_total = jnp.zeros((total, 1), jnp.float32)
    margins = jnp.zeros((total, table_cols), jnp.float32)
    for k in range(negatives):
        number = ids[:, k : k + 1]
        owner = number // store_rows
        local = number - owner * store_rows
        part = local // share
        inner = local - part * share
        chunk = inner // chunk_passages
        place = (chunk * shards + owner) * chunk_passages + inner - chunk * chunk_passages
        here = column == place
        sparse_neg = jnp.zeros((total, 1), jnp.float32)
        for g in range(groups):
            sparse_neg = sparse_neg + jnp.sum(
                jnp.where(here & (part == g), tables_ref[g], 0.0), axis=1, keepdims=True
            )
        named = passage == number
        dense_neg = jnp.sum(jnp.where(named, dense_all, 0.0), axis=1, keepdims=True)
        margin = pos_score - (sparse_neg * inv_vocab + dense_neg)
        coef = (margin - targets[:, k : k + 1]) / negatives
        weights = weights + jnp.where(named, coef, 0.0)
        coef_total = coef_total + coef
        margins = jnp.where(column == k, margin, margins)
    margin_buf[...] = margins
    linear = lax.axis_index("group") * shards + lax.axis_index("shard")
    margin_ref[...] = margin_buf[pl.ds(linear * own, own), :negatives]

    grad_query = (coef_total * positive_vec - dot(weights, store_vec, ((1,), (0,)))) * inv_root
    grad_positive = coef_total * query_vec * inv_root
    grad_store = dot(weights, query_vec, ((0,), (0,))) * (-inv_root)
    states = jnp.concatenate([query_cls, positive_cls, store_cls], axis=0)
    factors = jnp.concatenate([grad_query, grad_positive, grad_store], axis=0)
    grad_ref[...] = split_dot(states, factors)


def body(
    query_hidden,
    positive_hidden,
    passage_store,
    negative_ids,
    teacher_margins,
    transform_weight,
    vocab_weight,
    dense_weight,
):
    groups = lax.axis_size("group")
    shards = lax.axis_size("shard")
    devices = groups * shards
    bits = shards.bit_length() - 1
    queries, lq, width = query_hidden.shape
    store_rows, lp, _ = passage_store.shape
    negatives = negative_ids.shape[1]
    columns = vocab_weight.shape[1]
    share = store_rows // groups
    chunk_passages = min(CHUNK_PASSAGES, share)
    chunks = share // chunk_passages
    rows = 2 * (width // LANES) + 1
    rows += -rows % 8
    pooled = share * shards + shards * queries
    pooled += -pooled % 128
    total = devices * queries

    vmem = pl.BlockSpec(memory_space=pltpu.VMEM)
    hbm = pl.BlockSpec(memory_space=pl.ANY)
    dma = pltpu.SemaphoreType.DMA
    tables, cls_all, meta_all = pl.pallas_call(
        functools.partial(exchange_kernel, groups, shards, lq),
        out_shape=[
            jax.ShapeDtypeStruct((groups, total, pooled), jnp.float32),
            jax.ShapeDtypeStruct((shards, store_rows, width), jnp.bfloat16),
            jax.ShapeDtypeStruct((devices, queries, rows, LANES), jnp.float32),
        ],
        in_specs=[vmem] * 5 + [hbm] * 2,
        out_specs=[vmem] * 3,
        scratch_shapes=[
            pltpu.VMEM((store_rows, 8, width), jnp.bfloat16),
            pltpu.VMEM((share, lp, width), jnp.bfloat16),
            pltpu.VMEM((width, columns), jnp.bfloat16),
            pltpu.VMEM((shards, store_rows, width), jnp.bfloat16),
            pltpu.VMEM((devices, queries, rows, LANES), jnp.float32),
            pltpu.VMEM((shards, queries * (lq + lp), width), jnp.bfloat16),
            pltpu.VMEM((chunks, shards, chunk_passages * lp, width), jnp.bfloat16),
            pltpu.VMEM((groups, shards * queries, columns), jnp.float32),
            pltpu.VMEM((pooled, columns), jnp.float32),
            pltpu.VMEM((shards, total, pooled), jnp.float32),
            pltpu.VMEM((groups, total, pooled), jnp.float32),
            dma((3,)),
            dma((2 * (chunks + 2), shards, bits)),
            dma((2 * (chunks + 2), shards)),
            dma((devices,)),
            dma((devices,)),
            dma((groups,)),
            dma((groups,)),
            dma((shards,)),
            dma((shards,)),
            dma((groups,)),
            dma((groups,)),
        ],
        compiler_params=pltpu.CompilerParams(
            collective_id=0, has_side_effects=True, vmem_limit_bytes=56 * 1024 * 1024
        ),
        name="exchange",
    )(
        query_hidden,
        positive_hidden,
        negative_ids,
        teacher_margins,
        transform_weight,
        passage_store,
        vocab_weight,
    )
    return pl.pallas_call(
        functools.partial(
            loss_kernel, groups, shards, negatives, chunk_passages, columns * shards
        ),
        out_shape=[
            jax.ShapeDtypeStruct((queries, negatives), jnp.float32),
            jax.ShapeDtypeStruct((width, width), jnp.float32),
        ],
        in_specs=[hbm] * 4,
        out_specs=[vmem] * 2,
        scratch_shapes=[
            pltpu.VMEM((total, pooled), jnp.float32),
            pltpu.VMEM((groups, total, pooled), jnp.float32),
            pltpu.VMEM((shards, store_rows, width), jnp.bfloat16),
            pltpu.VMEM((total, rows, LANES), jnp.float32),
            pltpu.VMEM((width, width), jnp.bfloat16),
            dma((4,)),
        ],
        compiler_params=pltpu.CompilerParams(vmem_limit_bytes=56 * 1024 * 1024),
        name="loss",
    )(tables, cls_all, meta_all.reshape(total, rows, LANES), dense_weight)


def solution(mesh):
    in_specs = (
        P(("group", "shard"), None, None),
        P(("group", "shard"), None, None),
        P("shard", None, None),
        P(("group", "shard"), None),
        P(("group", "shard"), None),
        P(),
        P(None, "shard"),
        P(),
    )
    out_specs = (P(("group", "shard"), None), P())
    return jax.shard_map(body, mesh=mesh, in_specs=in_specs, out_specs=out_specs, check_vma=False)
```
